32 devices in a mesh: groups: 2 (over x), blk: 16 (over z, y, core).
Axes of the slice: x: 2, y: 2, z: 4, core: 2. Of those that a mesh axis runs over, the one named last changes fastest.
Arguments:
- hidden: bfloat16 [16384, 2048], P(('groups', 'blk')), parts along dimension 0, may hold values from -6 to 6
- kept_idx: int32 [32, 128], P(('groups', 'blk')), parts along dimension 0, may hold values from 0 to 511, as said below
- kept_count: int32 [32], P(('groups', 'blk')), parts along dimension 0, may hold values from 0 to 128, as said below
- router: bfloat16 [2048], replicated, may hold values from -0.125 to 0.125
- norm_gain: float32 [2048], replicated, may hold values from 0.25 to 1.75
- qk_gain: float32 [2, 64], replicated, may hold values from 1 to 7
- query_weight: bfloat16 [2048, 2048], P('blk'), may hold values from -1 to 1
- key_weight: bfloat16 [2048, 128], P('blk'), may hold values from -1 to 1
- value_weight: bfloat16 [2048, 128], P('blk'), may hold values from -0.125 to 0.125
- out_weight: bfloat16 [2048, 2048], P('blk'), may hold values from -0.375 to 0.375
Outputs:
- mixed: bfloat16 [16384, 2048], P(('groups', 'blk')), parts along dimension 0
The draws below stay inside these ranges and needn't reach their ends.
There are 2 independent parts, one for each index of `groups`. The reference program is written for one: setup_inputs(seed, part) draws one part's arguments, and reference() takes and returns one part's arrays. A program takes and returns all parts, laid end to end along the dimension named above; an argument that names none is the same for every part. Nothing has to cross between parts.
Inputs may be any that keep to these rules, and one draw needn't show every extreme that they name: `kept_count`: the counts sum to 1024; in every draw some shard's count is exactly 128. `kept_idx`: in row s the first kept_count[s] entries are distinct local token indices in increasing order; entries past the count are 0.
All inputs are finite; a program needn't handle non-finite values.
Results may differ from the reference program's by a relative error of at most 0.01.
Values may be sent and summed in bfloat16 or wider, within the bound.
A program may use at most 128 MiB of HBM per device.

```python
import math
import jax
import jax.numpy as jnp
from jax import lax

D = 2048
Q_HEADS = 32
KV_HEADS = 2
HEAD = 64
TOK_DEV = 512
KEEP_DEV = 64
CAP = 128
KEEP = 1024
TOKENS = 8192
N_BLK = 16


def lists_draw(key):
    base_key = jax.random.fold_in(key, 7)
    order_key, shift_key, rows_key = jax.random.split(base_key, 3)
    shard_order = jax.random.permutation(order_key, N_BLK)
    pair_total = N_BLK // 2
    shifts = jax.random.randint(shift_key, (pair_total,), 0, KEEP_DEV + 1)
    shifts = shifts.at[0].set(KEEP_DEV)
    pair_counts = jnp.concatenate([KEEP_DEV + shifts, KEEP_DEV - shifts]).astype(jnp.int32)
    counts = jnp.zeros((N_BLK,), jnp.int32).at[shard_order].set(pair_counts)
    row_keys = jax.random.split(rows_key, N_BLK)

    def one_shard(sub_key, kept_total):
        shuffled = jax.random.permutation(sub_key, TOK_DEV)
        placement = jnp.argsort(shuffled, stable=True)
        chosen = placement < kept_total
        slot_index = jnp.cumsum(chosen.astype(jnp.int32)) - 1
        target = jnp.where(chosen, slot_index, CAP)
        return jnp.zeros((CAP,), jnp.int32).at[target].set(jnp.arange(TOK_DEV, dtype=jnp.int32), mode='drop')
    lists = jax.vmap(one_shard)(row_keys, counts)
    return (counts, lists)


def draw_kept_count(key, part):
    return lists_draw(key)[0]


def draw_kept_idx(key, part):
    return lists_draw(key)[1]


def projection_pair(key):
    base_key = jax.random.fold_in(key, 11)
    key_part, query_part = jax.random.split(base_key, 2)
    group_size = Q_HEADS // KV_HEADS
    key_cols = jax.random.uniform(key_part, (D, KV_HEADS, HEAD), jnp.float32, -1.0, 1.0)
    fresh = jax.random.uniform(query_part, (D, KV_HEADS, group_size, HEAD), jnp.float32, -1.0, 1.0)
    query_cols = fresh
    return (query_cols.reshape(D, Q_HEADS * HEAD), key_cols.reshape(D, KV_HEADS * HEAD))


def draw_query_weight(key, part):
    return projection_pair(key)[0].astype(jnp.bfloat16)


def draw_key_weight(key, part):
    return projection_pair(key)[1].astype(jnp.bfloat16)


def draw_qk_gain(key, part):
    base_key = jax.random.fold_in(key, 23)
    return jax.random.uniform(base_key, (2, HEAD), jnp.float32, 1.0, 2.0)


def block_levels(rng, dims, cuts, smallest, high):
    def one(dim, shards_of):
        draws = jax.random.uniform(jax.random.fold_in(jax.random.fold_in(rng, 6), dim), (shards_of,), jnp.float32, smallest / len(cuts), high / len(cuts))
        return jnp.repeat(jnp.exp(draws), dims[dim] // shards_of).reshape((-1,) + (1,) * (len(dims) - dim - 1))

    loudness = one(*cuts[0])
    for cut in cuts[1:]:
        loudness = loudness * one(*cut)
    return loudness


def noise(own_key, dims, width, most, shards=(), kind=jnp.bfloat16):
    values = width * jax.random.normal(own_key, dims, jnp.float32)
    if shards:
        values = values * block_levels(own_key, dims, shards, -0.22, 0.18)
    return jnp.clip(values, -most, most).astype(kind)


def setup_inputs(seed: int = 0, part: int = 0) -> dict:
    streams_of = jax.random.split(jax.random.key(seed), 11)
    part_keys = jax.random.split(jax.random.fold_in(streams_of[10], part), 11)
    return {
        "hidden": noise(part_keys[0], (TOKENS, D), 1.0, 6.0, ((0, 16),)),
        "kept_idx": draw_kept_idx(jax.random.fold_in(jax.random.fold_in(streams_of[10], part), 71), part),
        "kept_count": draw_kept_count(jax.random.fold_in(jax.random.fold_in(streams_of[10], part), 71), part),
        "router": noise(streams_of[3], (D,), D ** -0.5, 0.125),
        "norm_gain": jnp.clip(1.0 + 0.15 * jax.random.normal(streams_of[4], (D,), jnp.float32), 0.25, 1.75),
        "qk_gain": draw_qk_gain(jax.random.fold_in(streams_of[10], 71), part),
        "query_weight": draw_query_weight(jax.random.fold_in(streams_of[10], 71), part),
        "key_weight": draw_key_weight(jax.random.fold_in(streams_of[10], 71), part),
        "value_weight": noise(streams_of[8], (D, KV_HEADS * HEAD), D ** -0.5, 0.125, ((0, 16),)),
        "out_weight": noise(streams_of[9], (Q_HEADS * HEAD, D), (HEAD * 4) ** -0.5, 0.375, ((0, 16),)),
    }


norm_eps = 1e-06
rope_base = 1000000.0

def rms_scale(values, scales):
    return values * lax.rsqrt(lax.optimization_barrier(jnp.mean(values * values, axis=-1, keepdims=True)) + norm_eps) * scales

def rotate(values, angles):
    half_size = values.shape[-1] // 2
    lower_half = values[..., :half_size]
    upper_half = values[..., half_size:]
    cosine = jnp.cos(angles)
    sine_part = jnp.sin(angles)
    return jnp.concatenate([lower_half * cosine - upper_half * sine_part, upper_half * cosine + lower_half * sine_part], axis=-1)

def prepare(query_lin, key_lin, value_lin, qk_gain, positions):
    count_rows = positions.shape[0]
    half_size = HEAD // 2
    rotation_rates = rope_base ** (-(jnp.arange(half_size, dtype=jnp.float32) * 2.0 / HEAD))
    angles = (positions.astype(jnp.float32)[:, None] * rotation_rates[None, :])[:, None, :]
    query_heads = rms_scale(query_lin.reshape(count_rows, Q_HEADS, HEAD), qk_gain[0])
    key_heads = rms_scale(key_lin.reshape(count_rows, KV_HEADS, HEAD), qk_gain[1])
    query_heads = rotate(query_heads, angles).astype(jnp.bfloat16)
    key_heads = rotate(key_heads, angles).astype(jnp.bfloat16)
    value_heads = value_lin.reshape(count_rows, KV_HEADS, HEAD).astype(jnp.bfloat16)
    query_heads = query_heads.reshape(count_rows, KV_HEADS, Q_HEADS // KV_HEADS, HEAD)
    return (query_heads, key_heads, value_heads)

def reference(hidden, kept_idx, kept_count, router, norm_gain, qk_gain, query_weight, key_weight, value_weight, out_weight):
    starts = jnp.cumsum(kept_count) - kept_count
    slot_ids = jnp.arange(CAP, dtype=jnp.int32)
    is_valid = slot_ids[None, :] < kept_count[:, None]
    rank_grid = jnp.where(is_valid, starts[:, None] + slot_ids[None, :], KEEP).astype(jnp.int32)
    positions = (jnp.arange(N_BLK, dtype=jnp.int32)[:, None] * TOK_DEV + kept_idx).astype(jnp.int32)
    by_rank = jnp.zeros((KEEP,), jnp.int32).at[rank_grid.reshape(-1)].set(positions.reshape(-1), mode='drop')
    token_rows = hidden[by_rank]
    gate_value = jax.nn.sigmoid(jnp.dot(token_rows, router, preferred_element_type=jnp.float32))
    normed = rms_scale(token_rows.astype(jnp.float32), norm_gain).astype(jnp.bfloat16)
    query_lin = jnp.dot(normed, query_weight, preferred_element_type=jnp.float32)
    key_lin = jnp.dot(normed, key_weight, preferred_element_type=jnp.float32)
    value_lin = jnp.dot(normed, value_weight, preferred_element_type=jnp.float32)
    query_heads, key_heads, value_heads = prepare(query_lin, key_lin, value_lin, qk_gain, by_rank)
    keys_wide = key_heads.astype(jnp.float32)
    values_wide = value_heads.astype(jnp.float32)
    block_rows = math.gcd(KEEP, 256)
    all_ranks = jnp.arange(KEEP, dtype=jnp.int32)
    score_scale = 1.0 / math.sqrt(HEAD)

    def one_block(block_start):
        query_block = lax.dynamic_slice_in_dim(query_heads, block_start, block_rows, 0).astype(jnp.float32)
        scores = jnp.einsum('agch,bgh->gcab', query_block, keys_wide) * score_scale
        query_ranks = block_start + jnp.arange(block_rows, dtype=jnp.int32)
        allowed = all_ranks[None, :] <= query_ranks[:, None]
        masked = jnp.where(allowed, scores, -1e+30)
        row_top = lax.optimization_barrier(jnp.max(masked, axis=-1, keepdims=True))
        weights = jnp.where(allowed, jnp.exp(masked - row_top), 0.0)
        denominator = lax.optimization_barrier(jnp.sum(weights, axis=-1))
        rounded = lax.optimization_barrier(weights.astype(jnp.bfloat16)).astype(jnp.float32)
        mixture = jnp.einsum('gcab,bgh->gcah', rounded, values_wide) / denominator[..., None]
        return mixture.transpose(2, 0, 1, 3).reshape(block_rows, Q_HEADS * HEAD).astype(jnp.bfloat16)
    block_starts = (jnp.arange(KEEP // block_rows, dtype=jnp.int32) * block_rows).astype(jnp.int32)
    attended = lax.map(one_block, block_starts).reshape(KEEP, Q_HEADS * HEAD)
    update = jnp.dot(attended, out_weight, preferred_element_type=jnp.float32).astype(jnp.bfloat16)
    final = (token_rows.astype(jnp.float32) + gate_value[:, None] * update.astype(jnp.float32)).astype(jnp.bfloat16)
    return hidden.at[by_rank].set(final)
```

```python
import functools
import math

import jax
import jax.numpy as jnp
from jax import lax
from jax.experimental import pallas as pl
from jax.experimental.pallas import tpu as pltpu
from jax.sharding import PartitionSpec as P

Q_HEADS = 32
KV_HEADS = 2
HEAD = 64
TOK_DEV = 512
KEEP_DEV = 64
CAP = 128
MESH = pl.DeviceIdType.MESH
VM = pl.BlockSpec(memory_space=pltpu.VMEM)


norm_eps = 1e-06
rope_base = 1000000.0


def rms_scale(values, scales):
    return values * lax.rsqrt(jnp.mean(values * values, axis=-1, keepdims=True) + norm_eps) * scales


def rotate(values, angles):
    half_size = values.shape[-1] // 2
    lower_half = values[..., :half_size]
    upper_half = values[..., half_size:]
    cosine = jnp.cos(angles)
    sine_part = jnp.sin(angles)
    return jnp.concatenate(
        [
            lower_half * cosine - upper_half * sine_part,
            upper_half * cosine + lower_half * sine_part,
        ],
        axis=-1,
    )


def greet(peers):
    barrier = pltpu.get_barrier_semaphore()
    for peer in peers:
        pl.semaphore_signal(barrier, inc=1, device_id={"blk": peer}, device_id_type=MESH)
    pl.semaphore_wait(barrier, len(peers))


def exchange_kernel(n, split, *refs):
    count = len(split)
    ins, outs = refs[:count], refs[count : 2 * count]
    send_sem, recv_sem = refs[2 * count :]
    me = lax.axis_index("blk")

    def block(i, d):
        if not split[i]:
            return ins[i]
        width = outs[i].shape[-1]
        return ins[i].at[:, pl.ds(pl.multiple_of(d * width, width), width)]

    greet([lax.rem(me + o, n) for o in range(1, n)])
    copies = []
    for o in range(1, n):
        dest = lax.rem(me + o, n)
        for i in range(count):
            copy = pltpu.make_async_remote_copy(
                src_ref=block(i, dest),
                dst_ref=outs[i].at[me],
                send_sem=send_sem.at[i, o],
                recv_sem=recv_sem.at[i, o],
                device_id={"blk": dest},
                device_id_type=MESH,
            )
            copy.start()
            copies.append(copy)
    for i in range(count):
        outs[i][me] = block(i, me)[...]
    for o in range(1, n):
        source = lax.rem(me + n - o, n)
        for i in range(count):
            pltpu.make_async_remote_copy(
                src_ref=block(i, me),
                dst_ref=outs[i].at[source],
                send_sem=send_sem.at[i, o],
                recv_sem=recv_sem.at[i, o],
                device_id={"blk": source},
                device_id_type=MESH,
            ).wait_recv()
    for copy in copies:
        copy.wait_send()


def exchange(n, arrays, split, collective_id):
    outs = []
    for a, s in zip(arrays, split):
        shape = (n, a.shape[0], a.shape[1] // n if s else a.shape[1])
        outs.append(jax.ShapeDtypeStruct(shape, a.dtype))
    return pl.pallas_call(
        functools.partial(exchange_kernel, n, split),
        out_shape=outs,
        in_specs=[VM] * len(arrays),
        out_specs=[VM] * len(arrays),
        scratch_shapes=[
            pltpu.SemaphoreType.DMA((len(arrays), n)),
            pltpu.SemaphoreType.DMA((len(arrays), n)),
        ],
        compiler_params=pltpu.CompilerParams(collective_id=collective_id, has_side_effects=True),
    )(*arrays)


def scatter_sum_kernel(n, pieces, classes, *refs):
    kinds = len(classes)
    ins, outs = refs[:pieces], refs[pieces : pieces + kinds]
    scratch = refs[pieces + kinds :]
    chips = n // 2
    arm = chips // 2
    me = lax.axis_index("blk")
    chip, core = me // 2, me % 2
    side, row = chip % 2, chip // 2
    place = row * (1 - side) + (chips - 1 - row) * side

    def device(position, on_core):
        q = lax.rem(position + 2 * chips, chips)
        far = q // arm
        chip_id = 2 * (q * (1 - far) + (chips - 1 - q) * far) + far
        return chip_id * 2 + on_core

    partner = chip * 2 + 1 - core
    ahead, behind = device(place + 1, core), device(place - 1, core)
    greet([partner, ahead, behind])

    bufs = [scratch[8 * i : 8 * i + 8] for i in range(kinds)]
    units = [(i, u) for i, c in enumerate(classes) for u in range(c[1])]

    def target(step, u):
        return place - 1 - step if u % 2 == 0 else place + 1 + step

    def pair_copy(step, i, u):
        pair_out, pair_in, _, _, ps, pr, _, _ = bufs[i]
        return pltpu.make_async_remote_copy(
            src_ref=pair_out.at[step, u],
            dst_ref=pair_in.at[step, u],
            send_sem=ps.at[step, u],
            recv_sem=pr.at[step, u],
            device_id={"blk": partner},
            device_id_type=MESH,
        )

    def ring_copy(step, i, u):
        _, _, ring_out, ring_in, _, _, rs, rr = bufs[i]
        return pltpu.make_async_remote_copy(
            src_ref=ring_out.at[step, u],
            dst_ref=ring_in.at[step, u],
            send_sem=rs.at[step, u],
            recv_sem=rr.at[step, u],
            device_id={"blk": ahead if u % 2 == 0 else behind},
            device_id_type=MESH,
        )

    def pair_send(step):
        for i, u in units:
            chunk = classes[i][0]
            bufs[i][0][step, u] = chunk(ins, device(target(step, u), 1 - core), u).astype(jnp.bfloat16)
            pair_copy(step, i, u).start()

    pair_send(0)
    for step in range(chips):
        if step + 1 < chips:
            pair_send(step + 1)
        for i, u in units:
            chunk = classes[i][0]
            total = chunk(ins, device(target(step, u), core), u)
            pair_copy(step, i, u).wait_recv()
            total = total + bufs[i][1][step, u].astype(jnp.float32)
            if step > 0:
                ring_copy(step - 1, i, u).wait_recv()
                total = total + bufs[i][3][step - 1, u].astype(jnp.float32)
            if step + 1 < chips:
                bufs[i][2][step, u] = total.astype(jnp.bfloat16)
                ring_copy(step, i, u).start()
            else:
                outs[i][u] = total.astype(outs[i].dtype)
    for step in range(chips):
        for i, u in units:
            pair_copy(step, i, u).wait_send()
            if step + 1 < chips:
                ring_copy(step, i, u).wait_send()


def scatter_sum(n, arrays, classes, out_types, collective_id):
    chips = n // 2
    scratch = []
    for _, u, r, c in classes:
        scratch += [
            pltpu.VMEM((chips, u, r, c), jnp.bfloat16),
            pltpu.VMEM((chips, u, r, c), jnp.bfloat16),
            pltpu.VMEM((chips - 1, u, r, c), jnp.bfloat16),
            pltpu.VMEM((chips - 1, u, r, c), jnp.bfloat16),
            pltpu.SemaphoreType.DMA((chips, u)),
            pltpu.SemaphoreType.DMA((chips, u)),
            pltpu.SemaphoreType.DMA((chips - 1, u)),
            pltpu.SemaphoreType.DMA((chips - 1, u)),
        ]
    return pl.pallas_call(
        functools.partial(scatter_sum_kernel, n, len(arrays), classes),
        out_shape=[
            jax.ShapeDtypeStruct((u, r, c), t) for (_, u, r, c), t in zip(classes, out_types)
        ],
        in_specs=[VM] * len(arrays),
        out_specs=[VM] * len(classes),
        scratch_shapes=scratch,
        compiler_params=pltpu.CompilerParams(collective_id=collective_id, has_side_effects=True),
    )(*arrays)


def attention_kernel(heads, block, q_ref, k_ref, v_ref, o_ref):
    total = q_ref.shape[0]
    for begin in range(0, total, block):
        end = begin + block
        keys = k_ref[:end, :]
        values = v_ref[:end, :]
        row = lax.broadcasted_iota(jnp.int32, (block, end), 0) + begin
        col = lax.broadcasted_iota(jnp.int32, (block, end), 1)
        for h in range(heads):
            query = q_ref[begin:end, h * HEAD : (h + 1) * HEAD]
            scores = lax.dot_general(
                query, keys, (((1,), (1,)), ((), ())), preferred_element_type=jnp.float32
            ) * (1.0 / math.sqrt(HEAD))
            scores = jnp.where(col <= row, scores, -1e30)
            top = jnp.max(scores, axis=-1, keepdims=True)
            weights = jnp.exp(scores - top)
            denominator = jnp.sum(weights, axis=-1, keepdims=True)
            mix = jnp.dot(weights.astype(jnp.bfloat16), values, preferred_element_type=jnp.float32)
            o_ref[begin:end, h * HEAD : (h + 1) * HEAD] = (mix / denominator).astype(o_ref.dtype)


def body(
    n,
    hidden,
    kept_idx,
    kept_count,
    router,
    norm_gain,
    qk_gain,
    query_weight,
    key_weight,
    value_weight,
    out_weight,
):
    device = lax.axis_index("blk")
    tokens, width = hidden.shape
    cap = kept_idx.shape[1]
    part = width // n
    slots = jnp.arange(cap, dtype=jnp.int32)
    token_rows = hidden[kept_idx[0]]
    gate_value = jax.nn.sigmoid(jnp.dot(token_rows, router, preferred_element_type=jnp.float32))
    normed = rms_scale(token_rows.astype(jnp.float32), norm_gain).astype(jnp.bfloat16)
    meta = jnp.concatenate(
        [kept_idx, jnp.broadcast_to(kept_count[:, None], (7, cap))], axis=0
    ).astype(jnp.int32)
    rows_by_shard, metas = exchange(n, (normed, meta), (True, False), 1)
    counts = metas[:, 1, 0]
    lists = metas[:, 0, :]
    starts = jnp.cumsum(counts) - counts
    valid = slots[None, :] < counts[:, None]
    keep = n * KEEP_OF(tokens)
    ranks = jnp.where(valid, starts[:, None] + slots[None, :], keep).reshape(-1)
    places = (jnp.arange(n, dtype=jnp.int32)[:, None] * tokens + lists).reshape(-1)
    sel = ranks[None, :] == jnp.arange(keep, dtype=jnp.int32)[:, None]
    positions = jnp.sum(jnp.where(sel, places[None, :], 0), axis=1)
    rows = jnp.dot(
        sel.astype(jnp.bfloat16),
        rows_by_shard.reshape(n * cap, part),
        preferred_element_type=jnp.float32,
    ).astype(jnp.bfloat16)
    own = keep // n
    q_cols = Q_HEADS * HEAD // n
    kv_cols = 2 * KV_HEADS * HEAD
    q_units = 4
    q_rows = keep // q_units
    kv_rows = own // 2
    kv_weight = jnp.concatenate([key_weight, value_weight], axis=1)

    def query_chunk(ins, dest, u):
        cols = pl.ds(pl.multiple_of(dest * q_cols, q_cols), q_cols)
        return jnp.dot(
            ins[0][u * q_rows : (u + 1) * q_rows, :],
            ins[1][:, cols],
            preferred_element_type=jnp.float32,
        )

    def kv_chunk(ins, dest, u):
        at = pl.ds(pl.multiple_of(dest * own + u * kv_rows, kv_rows), kv_rows)
        return jnp.dot(ins[0][at, :], ins[2][...], preferred_element_type=jnp.float32)

    query_lin, kv_lin = scatter_sum(
        n,
        (rows, query_weight, kv_weight),
        ((query_chunk, q_units, q_rows, q_cols), (kv_chunk, 2, kv_rows, kv_cols)),
        (jnp.float32, jnp.float32),
        2,
    )
    heads = Q_HEADS // n
    query_lin = query_lin.reshape(keep, heads, HEAD)
    kv_lin = kv_lin.reshape(own, 2 * KV_HEADS, HEAD)
    half_size = HEAD // 2
    rotation_rates = rope_base ** (-(jnp.arange(half_size, dtype=jnp.float32) * 2.0 / HEAD))
    angles = (positions.astype(jnp.float32)[:, None] * rotation_rates[None, :])[:, None, :]
    query_heads = rotate(rms_scale(query_lin, qk_gain[0]), angles).astype(jnp.bfloat16)
    own_angles = lax.dynamic_slice_in_dim(angles, device * own, own, 0)
    key_heads = rotate(rms_scale(kv_lin[:, :KV_HEADS], qk_gain[1]), own_angles).astype(jnp.bfloat16)
    value_heads = kv_lin[:, KV_HEADS:].astype(jnp.bfloat16)
    own_kv = jnp.concatenate(
        [key_heads.reshape(own, KV_HEADS * HEAD), value_heads.reshape(own, KV_HEADS * HEAD)], axis=1
    )
    (all_kv,) = exchange(n, (own_kv,), (False,), 3)
    all_kv = all_kv.reshape(keep, 2 * KV_HEADS, HEAD)
    group = device * heads // (Q_HEADS // KV_HEADS)
    keys = lax.dynamic_index_in_dim(all_kv, group, 1, keepdims=False)
    values = lax.dynamic_index_in_dim(all_kv, KV_HEADS + group, 1, keepdims=False)
    attended = pl.pallas_call(
        functools.partial(attention_kernel, heads, math.gcd(keep, 256)),
        out_shape=jax.ShapeDtypeStruct((keep, q_cols), jnp.bfloat16),
        in_specs=[VM] * 3,
        out_specs=VM,
    )(query_heads.reshape(keep, q_cols), keys, values)
    padded = lax.dot_general(
        sel.astype(jnp.bfloat16), attended, (((0,), (0,)), ((), ())), preferred_element_type=jnp.float32
    ).astype(jnp.bfloat16)
    out_units = 4
    out_rows = cap // out_units

    def out_chunk(ins, dest, u):
        at = pl.ds(pl.multiple_of(dest * cap + u * out_rows, out_rows), out_rows)
        return jnp.dot(ins[0][at, :], ins[1][...], preferred_element_type=jnp.float32)

    (update,) = scatter_sum(
        n,
        (padded, out_weight),
        ((out_chunk, out_units, out_rows, width),),
        (jnp.bfloat16,),
        4,
    )
    update = update.reshape(cap, width).astype(jnp.float32)
    final = (token_rows.astype(jnp.float32) + gate_value[:, None] * update).astype(jnp.bfloat16)
    put = (kept_idx == jnp.arange(tokens, dtype=jnp.int32)[:, None]) & (slots[None, :] < kept_count[0])
    placed = jnp.dot(put.astype(jnp.bfloat16), final, preferred_element_type=jnp.float32)
    return jnp.where(jnp.any(put, axis=1)[:, None], placed.astype(jnp.bfloat16), hidden)


def KEEP_OF(tokens):
    return tokens * KEEP_DEV // TOK_DEV


def attend(query_heads, query_ranks, key_block, value_block, key_ranks, state):
    prev_top, prev_total, prev_acc = state
    length = key_block.shape[0]
    keys_split = key_block.reshape(length, KV_HEADS, HEAD)
    values_split = value_block.reshape(length, KV_HEADS, HEAD)
    scores = jnp.einsum(
        "agch,bgh->gcab", query_heads, keys_split, preferred_element_type=jnp.float32
    ) * (1.0 / math.sqrt(HEAD))
    allowed = key_ranks[None, :] <= query_ranks[:, None]
    masked = jnp.where(allowed, scores, -1e30)
    new_top = jnp.maximum(prev_top, jnp.max(masked, axis=-1))
    weights = jnp.where(allowed, jnp.exp(masked - new_top[..., None]), 0.0)
    factor = jnp.exp(prev_top - new_top)
    new_total = prev_total * factor + jnp.sum(weights, axis=-1)
    new_acc = prev_acc * factor[..., None] + jnp.einsum(
        "gcab,bgh->gcah",
        weights.astype(jnp.bfloat16),
        values_split,
        preferred_element_type=jnp.float32,
    )
    return (new_top, new_total, new_acc)


def make_fold(query_heads, query_ranks, rank_of, state, pieces):
    key_piece, value_piece = pieces
    length = key_piece.shape[0]

    def inner(block_turn, inner_state):
        block_start = block_turn * 512
        key_block = lax.dynamic_slice_in_dim(key_piece, block_start, 512, 0)
        value_block = lax.dynamic_slice_in_dim(value_piece, block_start, 512, 0)
        key_ranks = rank_of(block_start + jnp.arange(512, dtype=jnp.int32))
        return attend(query_heads, query_ranks, key_block, value_block, key_ranks, inner_state)

    return lax.fori_loop(0, length // 512, inner, state)


def wide_body(
    hidden,
    kept_idx,
    kept_count,
    router,
    norm_gain,
    qk_gain,
    query_weight,
    key_weight,
    value_weight,
    out_weight,
):
    shard_count = lax.axis_size("blk")
    device = lax.axis_index("blk")
    width = hidden.shape[1]
    all_lists, all_counts = (
        lax.all_gather(kept_idx, "blk", axis=0, tiled=True),
        lax.all_gather(kept_count, "blk", axis=0, tiled=True),
    )
    starts = jnp.cumsum(all_counts) - all_counts
    own_start = starts[device]
    own_count = all_counts[device]
    list_slots = jnp.arange(CAP, dtype=jnp.int32)
    is_valid = list_slots < own_count
    token_rows = hidden[kept_idx[0]]
    gate_value = jax.nn.sigmoid(jnp.dot(token_rows, router, preferred_element_type=jnp.float32))
    slot_count = (CAP + shard_count - 1) // shard_count
    outgoing = jnp.where(is_valid[:, None], token_rows, jnp.zeros_like(token_rows))
    outgoing = jnp.roll(outgoing.reshape(slot_count, shard_count, width), own_start, axis=1)
    incoming = lax.all_to_all(outgoing, "blk", split_axis=1, concat_axis=1, tiled=True)
    query_ranks = device + jnp.arange(KEEP_DEV, dtype=jnp.int32) * shard_count
    source_ends = starts + all_counts
    source = jnp.sum((source_ends[None, :] <= query_ranks[:, None]).astype(jnp.int32), axis=1)
    within = query_ranks - starts[source]
    flat_index = within // shard_count * shard_count + source
    kept_rows = incoming.reshape(slot_count * shard_count, width)[flat_index]
    positions = source * TOK_DEV + all_lists[source, within]
    row_total = kept_rows.shape[0]
    normed = rms_scale(kept_rows.astype(jnp.float32), norm_gain).astype(jnp.bfloat16)
    query_cols = Q_HEADS * HEAD
    kv_cols = KV_HEADS * HEAD
    full_query, full_key, full_value, full_out = (
        lax.all_gather(query_weight, "blk", axis=0, tiled=True),
        lax.all_gather(key_weight, "blk", axis=0, tiled=True),
        lax.all_gather(value_weight, "blk", axis=0, tiled=True),
        lax.all_gather(out_weight, "blk", axis=0, tiled=True),
    )
    query_lin = jnp.dot(normed, full_query, preferred_element_type=jnp.float32)
    key_lin = jnp.dot(normed, full_key, preferred_element_type=jnp.float32)
    value_lin = jnp.dot(normed, full_value, preferred_element_type=jnp.float32)
    half_size = HEAD // 2
    rotation_rates = rope_base ** (-(jnp.arange(half_size, dtype=jnp.float32) * 2.0 / HEAD))
    angles = (positions.astype(jnp.float32)[:, None] * rotation_rates[None, :])[:, None, :]
    query_heads = rotate(
        rms_scale(query_lin.reshape(row_total, Q_HEADS, HEAD), qk_gain[0]), angles
    ).astype(jnp.bfloat16)
    key_heads = rotate(
        rms_scale(key_lin.reshape(row_total, KV_HEADS, HEAD), qk_gain[1]), angles
    ).astype(jnp.bfloat16)
    query_heads = query_heads.reshape(row_total, KV_HEADS, Q_HEADS // KV_HEADS, HEAD)
    key_flat = key_heads.reshape(row_total, kv_cols)
    value_flat = value_lin.astype(jnp.bfloat16)
    group_size = Q_HEADS // KV_HEADS
    start_state = (
        jnp.full((KV_HEADS, group_size, row_total), -1e30, jnp.float32),
        jnp.zeros((KV_HEADS, group_size, row_total), jnp.float32),
        jnp.zeros((KV_HEADS, group_size, row_total, HEAD), jnp.float32),
    )

    def strided_rank(slots_seen):
        return slots_seen // KEEP_DEV + slots_seen % KEEP_DEV * shard_count

    final_top, final_total, final_acc = make_fold(
        query_heads,
        query_ranks,
        strided_rank,
        start_state,
        (
            lax.all_gather(key_flat, "blk", axis=0, tiled=True),
            lax.all_gather(value_flat, "blk", axis=0, tiled=True),
        ),
    )
    attended = (
        (final_acc / final_total[..., None])
        .transpose(2, 0, 1, 3)
        .reshape(row_total, query_cols)
        .astype(jnp.bfloat16)
    )
    update = jnp.dot(attended, full_out, preferred_element_type=jnp.float32)
    update = update.astype(jnp.bfloat16)
    slot_grid = (
        jnp.arange(slot_count, dtype=jnp.int32)[:, None] * shard_count
        + jnp.mod(device - starts, shard_count)[None, :]
    )
    back_valid = slot_grid < all_counts[None, :]
    local_place = (starts[None, :] + slot_grid - device) // shard_count
    clipped = jnp.where(back_valid, local_place, 0)
    back_rows = jnp.where(back_valid[..., None], update[clipped], jnp.zeros((), jnp.bfloat16))
    returned = lax.all_to_all(back_rows, "blk", split_axis=1, concat_axis=1, tiled=True)
    returned = jnp.roll(returned, -own_start, axis=1).reshape(slot_count * shard_count, width)
    final = (
        token_rows.astype(jnp.float32) + gate_value[:, None] * returned.astype(jnp.float32)
    ).astype(jnp.bfloat16)
    target = jnp.where(is_valid, kept_idx[0], TOK_DEV)
    return hidden.at[target].set(final, mode="drop")


def solution(mesh):
    placed = (
        P(("groups", "blk"), None),
        P(("groups", "blk"), None),
        P(("groups", "blk")),
        P(),
        P(),
        P(),
        P("blk", None),
        P("blk", None),
        P("blk", None),
        P("blk", None),
    )
    n = mesh.shape["blk"]
    by_heads = n % 4 == 0 and (Q_HEADS * HEAD // n) % 128 == 0
    step = functools.partial(body, n) if by_heads else wide_body
    return jax.shard_map(
        step, mesh=mesh, in_specs=placed, out_specs=P(("groups", "blk"), None), check_vma=False
    )
```

```python
import functools
import math

import jax
import jax.numpy as jnp
from jax import lax
from jax.experimental import pallas as pl
from jax.experimental.pallas import tpu as pltpu
from jax.sharding import PartitionSpec as P

Q_HEADS = 32
KV_HEADS = 2
HEAD = 64
TOK_DEV = 512
KEEP_DEV = 64
CAP = 128
MESH = pl.DeviceIdType.MESH
VM = pl.BlockSpec(memory_space=pltpu.VMEM)


norm_eps = 1e-06
rope_base = 1000000.0


def rms_scale(values, scales):
    return values * lax.rsqrt(jnp.mean(values * values, axis=-1, keepdims=True) + norm_eps) * scales


def rotate(values, angles):
    half_size = values.shape[-1] // 2
    lower_half = values[..., :half_size]
    upper_half = values[..., half_size:]
    cosine = jnp.cos(angles)
    sine_part = jnp.sin(angles)
    return jnp.concatenate(
        [
            lower_half * cosine - upper_half * sine_part,
            upper_half * cosine + lower_half * sine_part,
        ],
        axis=-1,
    )


def greet(peers):
    barrier = pltpu.get_barrier_semaphore()
    for peer in peers:
        pl.semaphore_signal(barrier, inc=1, device_id={"blk": peer}, device_id_type=MESH)
    pl.semaphore_wait(barrier, len(peers))


def spread_kernel(n, hidden_ref, idx_ref, count_ref, gain_ref, out_ref, metas_ref, rows_ref, x_buf, meta_buf, send_sem, recv_sem):
    me = lax.axis_index("blk")
    part = out_ref.shape[-1]
    barrier = pltpu.get_barrier_semaphore()
    for o in range(1, n):
        pl.semaphore_signal(
            barrier, inc=1, device_id={"blk": lax.rem(me + o, n)}, device_id_type=MESH
        )
    tokens, cap = hidden_ref.shape[0], idx_ref.shape[1]
    pick = lax.broadcasted_iota(jnp.int32, (tokens, cap), 0) == idx_ref[...]
    rows = lax.dot_general(
        pick.astype(jnp.float32).astype(jnp.bfloat16),
        hidden_ref[...],
        (((0,), (0,)), ((), ())),
        preferred_element_type=jnp.float32,
    )
    rows_ref[...] = rows.astype(jnp.bfloat16)
    x_buf[...] = rms_scale(rows, gain_ref[...]).astype(jnp.bfloat16)
    line = lax.broadcasted_iota(jnp.int32, meta_buf.shape, 0)
    meta_buf[...] = jnp.where(line == 0, idx_ref[...], count_ref[...])

    def copies(o, dest, place):
        cols = pl.ds(pl.multiple_of(dest * part, part), part)
        pairs = ((x_buf.at[:, cols], out_ref), (meta_buf, metas_ref))
        return [
            pltpu.make_async_remote_copy(
                src_ref=src,
                dst_ref=dst.at[place],
                send_sem=send_sem.at[i, o],
                recv_sem=recv_sem.at[i, o],
                device_id={"blk": dest},
                device_id_type=MESH,
            )
            for i, (src, dst) in enumerate(pairs)
        ]

    pl.semaphore_wait(barrier, n - 1)
    started = []
    for o in range(1, n):
        for copy in copies(o, lax.rem(me + o, n), me):
            copy.start()
            started.append(copy)
    out_ref[me] = x_buf[:, pl.ds(pl.multiple_of(me * part, part), part)]
    metas_ref[me] = meta_buf[...]
    for o in range(1, n):
        source = lax.rem(me + n - o, n)
        for copy in copies(o, source, source):
            copy.wait_recv()
    for copy in started:
        copy.wait_send()


def spread(n, hidden, kept_idx, kept_count, norm_gain):
    width, cap = hidden.shape[1], kept_idx.shape[1]
    return pl.pallas_call(
        functools.partial(spread_kernel, n),
        out_shape=[
            jax.ShapeDtypeStruct((n, cap, width // n), jnp.bfloat16),
            jax.ShapeDtypeStruct((n, 8, cap), jnp.int32),
            jax.ShapeDtypeStruct((cap, width), jnp.bfloat16),
        ],
        in_specs=[VM] * 4,
        out_specs=[VM] * 3,
        scratch_shapes=[
            pltpu.VMEM((cap, width), jnp.bfloat16),
            pltpu.VMEM((8, cap), jnp.int32),
            pltpu.SemaphoreType.DMA((2, n)),
            pltpu.SemaphoreType.DMA((2, n)),
        ],
        compiler_params=pltpu.CompilerParams(collective_id=1, has_side_effects=True),
    )(hidden, kept_idx, kept_count.reshape(1, 1), norm_gain.reshape(1, width))


class Ring:
    def __init__(self, n):
        self.chips = n // 2
        self.arm = self.chips // 2
        self.me = lax.axis_index("blk")
        self.chip, self.core = self.me // 2, self.me % 2
        side, row = self.chip % 2, self.chip // 2
        self.place = row * (1 - side) + (self.chips - 1 - row) * side
        self.partner = self.chip * 2 + 1 - self.core
        self.ahead = self.device(self.place + 1, self.core)
        self.behind = self.device(self.place - 1, self.core)

    def device(self, position, on_core):
        q = lax.rem(position + 2 * self.chips, self.chips)
        far = q // self.arm
        chip_id = 2 * (q * (1 - far) + (self.chips - 1 - q) * far) + far
        return chip_id * 2 + on_core

    def target(self, step, u):
        return self.place - 1 - step if u % 2 == 0 else self.place + 1 + step


class RingSum:
    def __init__(self, ring, chunk, units, bufs, finish):
        self.ring, self.chunk, self.units, self.bufs, self.finish = ring, chunk, units, bufs, finish

    @staticmethod
    def scratch(chips, u, r, c):
        return [
            pltpu.VMEM((chips, u, r, c), jnp.bfloat16),
            pltpu.VMEM((chips, u, r, c), jnp.bfloat16),
            pltpu.VMEM((chips - 1, u, r, c), jnp.bfloat16),
            pltpu.VMEM((chips - 1, u, r, c), jnp.bfloat16),
            pltpu.SemaphoreType.DMA((chips, u)),
            pltpu.SemaphoreType.DMA((chips, u)),
            pltpu.SemaphoreType.DMA((chips - 1, u)),
            pltpu.SemaphoreType.DMA((chips - 1, u)),
        ]

    def copy(self, pair, step, u):
        pair_out, pair_in, ring_out, ring_in, ps, pr, rs, rr = self.bufs
        src, dst, ss, sr = (pair_out, pair_in, ps, pr) if pair else (ring_out, ring_in, rs, rr)
        to = self.ring.partner if pair else (self.ring.ahead if u % 2 == 0 else self.ring.behind)
        return pltpu.make_async_remote_copy(
            src_ref=src.at[step, u],
            dst_ref=dst.at[step, u],
            send_sem=ss.at[step, u],
            recv_sem=sr.at[step, u],
            device_id={"blk": to},
            device_id_type=MESH,
        )

    def pair_send(self, step):
        ring = self.ring
        for u in range(self.units):
            dest = ring.device(ring.target(step, u), 1 - ring.core)
            self.bufs[0][step, u] = self.chunk(dest, u).astype(jnp.bfloat16)
            self.copy(True, step, u).start()

    def advance(self, step):
        ring = self.ring
        for u in range(self.units):
            total = self.chunk(ring.device(ring.target(step, u), ring.core), u)
            self.copy(True, step, u).wait_recv()
            total = total + self.bufs[1][step, u].astype(jnp.float32)
            if step > 0:
                self.copy(False, step - 1, u).wait_recv()
                total = total + self.bufs[3][step - 1, u].astype(jnp.float32)
            if step + 1 < ring.chips:
                self.bufs[2][step, u] = total.astype(jnp.bfloat16)
                self.copy(False, step, u).start()
            else:
                self.finish(u, total)

    def drain(self):
        for step in range(self.ring.chips):
            for u in range(self.units):
                self.copy(True, step, u).wait_send()
                if step + 1 < self.ring.chips:
                    self.copy(False, step, u).wait_send()


def turn(values, cosine, sine, lane):
    swapped = jnp.where(lane % HEAD < HEAD // 2, pltpu.roll(values, 2 * HEAD - HEAD // 2, 1), pltpu.roll(values, HEAD // 2, 1))
    return values * cosine + swapped * sine


def attend_kernel(n, tokens, q_units, x_ref, metas_ref, wq_ref, wk_ref, wv_ref, gain_ref, rate_ref, padded_ref,
                  x_buf, pos_buf, kvp_buf, kv_lin, own_kv, all_kv, q_buf, att_buf, cos_buf, sin_buf,
                  kv_send, kv_recv, *bufs):
    ring = Ring(n)
    me, chips = ring.me, ring.chips
    barrier = pltpu.get_barrier_semaphore()
    for o in range(1, n):
        pl.semaphore_signal(
            barrier, inc=1, device_id={"blk": lax.rem(me + o, n)}, device_id_type=MESH
        )
    cap = x_ref.shape[1]
    keep = x_buf.shape[0]
    own = keep // n
    lanes = 2 * HEAD
    q_rows, kv_rows = keep // q_units, own // 2

    starts, counts = [], []
    start = jnp.zeros((1, cap), jnp.int32)
    for s in range(n):
        count = metas_ref[s, 1:2, :]
        starts.append(start)
        counts.append(count)
        start = start + count
    slot = lax.broadcasted_iota(jnp.int32, (1, cap), 1)
    block = 256
    for b in range(keep // block):
        rank = lax.broadcasted_iota(jnp.int32, (block, cap), 0) + b * block
        total = jnp.zeros((block, x_buf.shape[1]), jnp.float32)
        places = jnp.zeros((block, cap), jnp.float32)
        for s in range(n):
            rank_row = jnp.where(slot < counts[s], starts[s] + slot, keep)
            hit = rank == rank_row
            place_row = (metas_ref[s, 0:1, :] + s * tokens).astype(jnp.float32)
            places = places + jnp.where(hit, place_row, 0.0)
            total = total + jnp.dot(
                hit.astype(jnp.float32).astype(jnp.bfloat16), x_ref[s], preferred_element_type=jnp.float32
            )
        x_buf[b * block : (b + 1) * block, :] = total.astype(jnp.bfloat16)
        pos_buf[b * block : (b + 1) * block, :] = jnp.broadcast_to(
            jnp.sum(places, axis=1, keepdims=True), (block, lanes)
        )
    for g in range(KV_HEADS):
        weight = jnp.concatenate(
            [wk_ref[:, g * HEAD : (g + 1) * HEAD], wv_ref[:, g * HEAD : (g + 1) * HEAD]], axis=1
        )
        kvp_buf[:, g * lanes : (g + 1) * lanes] = jnp.dot(
            x_buf[...], weight, preferred_element_type=jnp.float32
        )

    def query_chunk(dest, u):
        cols = pl.ds(pl.multiple_of(dest * lanes, lanes), lanes)
        return jnp.dot(
            x_buf[u * q_rows : (u + 1) * q_rows, :], wq_ref[:, cols], preferred_element_type=jnp.float32
        )

    def kv_chunk(dest, u):
        return kvp_buf[pl.ds(pl.multiple_of(dest * own + u * kv_rows, kv_rows), kv_rows), :]

    def kv_finish(u, total):
        kv_lin[u * kv_rows : (u + 1) * kv_rows, :] = total

    lane = lax.broadcasted_iota(jnp.int32, (1, lanes), 1)
    sign = jnp.where(lane % HEAD < HEAD // 2, -1.0, 1.0)

    def query_finish(u, total):
        gain = jnp.concatenate([gain_ref[0:1, :], gain_ref[0:1, :]], axis=1)
        squares = total * total
        first = jnp.sum(jnp.where(lane < HEAD, squares, 0.0), axis=1, keepdims=True)
        second = jnp.sum(jnp.where(lane < HEAD, 0.0, squares), axis=1, keepdims=True)
        mean = jnp.where(lane < HEAD, first, second) * (1.0 / HEAD)
        values = total * lax.rsqrt(mean + norm_eps) * gain
        at = slice(u * q_rows, (u + 1) * q_rows)
        q_buf[at, :] = turn(values, cos_buf[at, :], sin_buf[at, :], lane).astype(jnp.bfloat16)

    kv_ring = RingSum(ring, kv_chunk, 2, bufs[:8], kv_finish)
    q_ring = RingSum(ring, query_chunk, q_units, bufs[8:], query_finish)

    def kv_copy(o, dest, place):
        return pltpu.make_async_remote_copy(
            src_ref=own_kv.at[dest * KV_HEADS // n],
            dst_ref=all_kv.at[place],
            send_sem=kv_send.at[o],
            recv_sem=kv_recv.at[o],
            device_id={"blk": dest},
            device_id_type=MESH,
        )

    def share():
        angle = pos_buf[pl.ds(pl.multiple_of(me * own, own), own), :] * rate_ref[...]
        cosine, sine = jnp.cos(angle), jnp.sin(angle) * sign
        gain = jnp.concatenate([gain_ref[1:2, :], gain_ref[1:2, :]], axis=1)
        for g in range(KV_HEADS):
            both = kv_lin[:, g * lanes : (g + 1) * lanes]
            mean = jnp.sum(jnp.where(lane < HEAD, both * both, 0.0), axis=1, keepdims=True) * (1.0 / HEAD)
            key = turn(both * lax.rsqrt(mean + norm_eps) * gain, cosine, sine, lane)
            own_kv[g] = jnp.where(lane < HEAD, key, both).astype(jnp.bfloat16)
        for o in range(1, n):
            kv_copy(o, lax.rem(me + o, n), me).start()
        all_kv[me] = own_kv[me * KV_HEADS // n]

    pl.semaphore_wait(barrier, n - 1)
    kv_ring.pair_send(0)
    kv_ring.pair_send(1)
    q_ring.pair_send(0)
    table = keep // chips
    for step in range(chips):
        for k in (2 * step, 2 * step + 1):
            if k < chips:
                kv_ring.advance(k)
                if k + 2 < chips:
                    kv_ring.pair_send(k + 2)
                if k + 1 == chips:
                    share()
        if step + 1 < chips:
            q_ring.pair_send(step + 1)
        rows = slice(step * table, (step + 1) * table)
        angle = pos_buf[rows, :] * rate_ref[...]
        cos_buf[rows, :] = jnp.cos(angle)
        sin_buf[rows, :] = jnp.sin(angle) * sign
        q_ring.advance(step)
    for o in range(1, n):
        source = lax.rem(me + n - o, n)
        kv_copy(o, source, source).wait_recv()

    for begin in range(0, keep, block):
        end = begin + block
        pairs = all_kv[: end // own].reshape(end, lanes)
        row = lax.broadcasted_iota(jnp.int32, (block, end), 0) + begin
        col = lax.broadcasted_iota(jnp.int32, (block, end), 1)
        both = q_buf[begin:end, :].astype(jnp.float32)
        mixes = []
        for h in range(2):
            query = jnp.where(lane < HEAD, both if h == 0 else pltpu.roll(both, HEAD, 1), 0.0)
            scores = lax.dot_general(
                query.astype(jnp.bfloat16), pairs, (((1,), (1,)), ((), ())), preferred_element_type=jnp.float32
            ) * (1.0 / math.sqrt(HEAD))
            scores = jnp.where(col <= row, scores, -1e30)
            top = jnp.max(scores, axis=-1, keepdims=True)
            weights = jnp.exp(scores - top)
            denominator = jnp.sum(weights, axis=-1, keepdims=True)
            mix = jnp.dot(weights.astype(jnp.bfloat16), pairs, preferred_element_type=jnp.float32)
            mixes.append(mix / denominator)
        att_buf[begin:end, :] = jnp.where(lane < HEAD, pltpu.roll(mixes[0], HEAD, 1), mixes[1]).astype(jnp.bfloat16)

    offset = lax.broadcasted_iota(jnp.int32, (cap, keep), 1) - lax.broadcasted_iota(jnp.int32, (cap, keep), 0)
    for s in range(n):
        hit = offset == starts[s][:, 0:1]
        padded_ref[s * cap : (s + 1) * cap, :] = jnp.dot(
            hit.astype(jnp.float32).astype(jnp.bfloat16), att_buf[...], preferred_element_type=jnp.float32
        ).astype(jnp.bfloat16)
    kv_ring.drain()
    q_ring.drain()
    for o in range(1, n):
        kv_copy(o, lax.rem(me + o, n), me).wait_send()


def attend_shards(n, tokens, keep, by_shard, metas, query_weight, key_weight, value_weight, qk_gain):
    cap, part = by_shard.shape[1:]
    lanes, own, chips, q_units = 2 * HEAD, keep // n, n // 2, 4
    half_size = HEAD // 2
    rates = rope_base ** (-(jnp.arange(half_size, dtype=jnp.float32) * 2.0 / HEAD))
    rates = jnp.tile(rates, lanes // half_size)[None, :]
    return pl.pallas_call(
        functools.partial(attend_kernel, n, tokens, q_units),
        out_shape=jax.ShapeDtypeStruct((n * cap, lanes), jnp.bfloat16),
        in_specs=[VM] * 7,
        out_specs=VM,
        scratch_shapes=[
            pltpu.VMEM((keep, part), jnp.bfloat16),
            pltpu.VMEM((keep, lanes), jnp.float32),
            pltpu.VMEM((keep, KV_HEADS * lanes), jnp.float32),
            pltpu.VMEM((own, KV_HEADS * lanes), jnp.float32),
            pltpu.VMEM((KV_HEADS, own, lanes), jnp.bfloat16),
            pltpu.VMEM((n, own, lanes), jnp.bfloat16),
            pltpu.VMEM((keep, lanes), jnp.bfloat16),
            pltpu.VMEM((keep, lanes), jnp.bfloat16),
            pltpu.VMEM((keep, lanes), jnp.float32),
            pltpu.VMEM((keep, lanes), jnp.float32),
            pltpu.SemaphoreType.DMA((n,)),
            pltpu.SemaphoreType.DMA((n,)),
        ]
        + RingSum.scratch(chips, 2, own // 2, KV_HEADS * lanes)
        + RingSum.scratch(chips, q_units, keep // q_units, lanes),
        compiler_params=pltpu.CompilerParams(collective_id=2, has_side_effects=True),
    )(by_shard, metas, query_weight, key_weight, value_weight, qk_gain, rates)


def deliver_kernel(n, units, padded_ref, weight_ref, out_ref, *bufs):
    ring = Ring(n)
    greet([ring.partner, ring.ahead, ring.behind])
    cap = padded_ref.shape[0] // n
    rows = cap // units

    def chunk(dest, u):
        at = pl.ds(pl.multiple_of(dest * cap + u * rows, rows), rows)
        return jnp.dot(padded_ref[at, :], weight_ref[...], preferred_element_type=jnp.float32)

    def finish(u, total):
        out_ref[u * rows : (u + 1) * rows, :] = total.astype(out_ref.dtype)

    summed = RingSum(ring, chunk, units, bufs, finish)
    summed.pair_send(0)
    for step in range(ring.chips):
        if step + 1 < ring.chips:
            summed.pair_send(step + 1)
        summed.advance(step)
    summed.drain()


def deliver(n, padded, out_weight):
    cap, width, units = padded.shape[0] // n, out_weight.shape[1], 4
    return pl.pallas_call(
        functools.partial(deliver_kernel, n, units),
        out_shape=jax.ShapeDtypeStruct((cap, width), jnp.bfloat16),
        in_specs=[VM] * 2,
        out_specs=VM,
        scratch_shapes=RingSum.scratch(n // 2, units, cap // units, width),
        compiler_params=pltpu.CompilerParams(collective_id=4, has_side_effects=True),
    )(padded, out_weight)


def body(
    n,
    hidden,
    kept_idx,
    kept_count,
    router,
    norm_gain,
    qk_gain,
    query_weight,
    key_weight,
    value_weight,
    out_weight,
):
    tokens = hidden.shape[0]
    cap = kept_idx.shape[1]
    keep = n * (tokens * KEEP_DEV // TOK_DEV)
    by_shard, metas, token_rows = spread(n, hidden, kept_idx, kept_count, norm_gain)
    padded = attend_shards(
        n, tokens, keep, by_shard, metas, query_weight, key_weight, value_weight, qk_gain
    )
    gate_value = jax.nn.sigmoid(jnp.dot(token_rows, router, preferred_element_type=jnp.float32))
    update = deliver(n, padded, out_weight).astype(jnp.float32)
    final = (token_rows.astype(jnp.float32) + gate_value[:, None] * update).astype(jnp.bfloat16)
    slots = jnp.arange(cap, dtype=jnp.int32)
    put = (kept_idx == jnp.arange(tokens, dtype=jnp.int32)[:, None]) & (slots[None, :] < kept_count[0])
    placed = jnp.dot(put.astype(jnp.bfloat16), final, preferred_element_type=jnp.float32)
    return jnp.where(jnp.any(put, axis=1)[:, None], placed.astype(jnp.bfloat16), hidden)


def attend(query_heads, query_ranks, key_block, value_block, key_ranks, state):
    prev_top, prev_total, prev_acc = state
    length = key_block.shape[0]
    keys_split = key_block.reshape(length, KV_HEADS, HEAD)
    values_split = value_block.reshape(length, KV_HEADS, HEAD)
    scores = jnp.einsum(
        "agch,bgh->gcab", query_heads, keys_split, preferred_element_type=jnp.float32
    ) * (1.0 / math.sqrt(HEAD))
    allowed = key_ranks[None, :] <= query_ranks[:, None]
    masked = jnp.where(allowed, scores, -1e30)
    new_top = jnp.maximum(prev_top, jnp.max(masked, axis=-1))
    weights = jnp.where(allowed, jnp.exp(masked - new_top[..., None]), 0.0)
    factor = jnp.exp(prev_top - new_top)
    new_total = prev_total * factor + jnp.sum(weights, axis=-1)
    new_acc = prev_acc * factor[..., None] + jnp.einsum(
        "gcab,bgh->gcah",
        weights.astype(jnp.bfloat16),
        values_split,
        preferred_element_type=jnp.float32,
    )
    return (new_top, new_total, new_acc)


def make_fold(query_heads, query_ranks, rank_of, state, pieces):
    key_piece, value_piece = pieces
    length = key_piece.shape[0]

    def inner(block_turn, inner_state):
        block_start = block_turn * 512
        key_block = lax.dynamic_slice_in_dim(key_piece, block_start, 512, 0)
        value_block = lax.dynamic_slice_in_dim(value_piece, block_start, 512, 0)
        key_ranks = rank_of(block_start + jnp.arange(512, dtype=jnp.int32))
        return attend(query_heads, query_ranks, key_block, value_block, key_ranks, inner_state)

    return lax.fori_loop(0, length // 512, inner, state)


def wide_body(
    hidden,
    kept_idx,
    kept_count,
    router,
    norm_gain,
    qk_gain,
    query_weight,
    key_weight,
    value_weight,
    out_weight,
):
    shard_count = lax.axis_size("blk")
    device = lax.axis_index("blk")
    width = hidden.shape[1]
    all_lists, all_counts = (
        lax.all_gather(kept_idx, "blk", axis=0, tiled=True),
        lax.all_gather(kept_count, "blk", axis=0, tiled=True),
    )
    starts = jnp.cumsum(all_counts) - all_counts
    own_start = starts[device]
    own_count = all_counts[device]
    list_slots = jnp.arange(CAP, dtype=jnp.int32)
    is_valid = list_slots < own_count
    token_rows = hidden[kept_idx[0]]
    gate_value = jax.nn.sigmoid(jnp.dot(token_rows, router, preferred_element_type=jnp.float32))
    slot_count = (CAP + shard_count - 1) // shard_count
    outgoing = jnp.where(is_valid[:, None], token_rows, jnp.zeros_like(token_rows))
    outgoing = jnp.roll(outgoing.reshape(slot_count, shard_count, width), own_start, axis=1)
    incoming = lax.all_to_all(outgoing, "blk", split_axis=1, concat_axis=1, tiled=True)
    query_ranks = device + jnp.arange(KEEP_DEV, dtype=jnp.int32) * shard_count
    source_ends = starts + all_counts
    source = jnp.sum((source_ends[None, :] <= query_ranks[:, None]).astype(jnp.int32), axis=1)
    within = query_ranks - starts[source]
    flat_index = within // shard_count * shard_count + source
    kept_rows = incoming.reshape(slot_count * shard_count, width)[flat_index]
    positions = source * TOK_DEV + all_lists[source, within]
    row_total = kept_rows.shape[0]
    normed = rms_scale(kept_rows.astype(jnp.float32), norm_gain).astype(jnp.bfloat16)
    query_cols = Q_HEADS * HEAD
    kv_cols = KV_HEADS * HEAD
    full_query, full_key, full_value, full_out = (
        lax.all_gather(query_weight, "blk", axis=0, tiled=True),
        lax.all_gather(key_weight, "blk", axis=0, tiled=True),
        lax.all_gather(value_weight, "blk", axis=0, tiled=True),
        lax.all_gather(out_weight, "blk", axis=0, tiled=True),
    )
    query_lin = jnp.dot(normed, full_query, preferred_element_type=jnp.float32)
    key_lin = jnp.dot(normed, full_key, preferred_element_type=jnp.float32)
    value_lin = jnp.dot(normed, full_value, preferred_element_type=jnp.float32)
    half_size = HEAD // 2
    rotation_rates = rope_base ** (-(jnp.arange(half_size, dtype=jnp.float32) * 2.0 / HEAD))
    angles = (positions.astype(jnp.float32)[:, None] * rotation_rates[None, :])[:, None, :]
    query_heads = rotate(
        rms_scale(query_lin.reshape(row_total, Q_HEADS, HEAD), qk_gain[0]), angles
    ).astype(jnp.bfloat16)
    key_heads = rotate(
        rms_scale(key_lin.reshape(row_total, KV_HEADS, HEAD), qk_gain[1]), angles
    ).astype(jnp.bfloat16)
    query_heads = query_heads.reshape(row_total, KV_HEADS, Q_HEADS // KV_HEADS, HEAD)
    key_flat = key_heads.reshape(row_total, kv_cols)
    value_flat = value_lin.astype(jnp.bfloat16)
    group_size = Q_HEADS // KV_HEADS
    start_state = (
        jnp.full((KV_HEADS, group_size, row_total), -1e30, jnp.float32),
        jnp.zeros((KV_HEADS, group_size, row_total), jnp.float32),
        jnp.zeros((KV_HEADS, group_size, row_total, HEAD), jnp.float32),
    )

    def strided_rank(slots_seen):
        return slots_seen // KEEP_DEV + slots_seen % KEEP_DEV * shard_count

    final_top, final_total, final_acc = make_fold(
        query_heads,
        query_ranks,
        strided_rank,
        start_state,
        (
            lax.all_gather(key_flat, "blk", axis=0, tiled=True),
            lax.all_gather(value_flat, "blk", axis=0, tiled=True),
        ),
    )
    attended = (
        (final_acc / final_total[..., None])
        .transpose(2, 0, 1, 3)
        .reshape(row_total, query_cols)
        .astype(jnp.bfloat16)
    )
    update = jnp.dot(attended, full_out, preferred_element_type=jnp.float32)
    update = update.astype(jnp.bfloat16)
    slot_grid = (
        jnp.arange(slot_count, dtype=jnp.int32)[:, None] * shard_count
        + jnp.mod(device - starts, shard_count)[None, :]
    )
    back_valid = slot_grid < all_counts[None, :]
    local_place = (starts[None, :] + slot_grid - device) // shard_count
    clipped = jnp.where(back_valid, local_place, 0)
    back_rows = jnp.where(back_valid[..., None], update[clipped], jnp.zeros((), jnp.bfloat16))
    returned = lax.all_to_all(back_rows, "blk", split_axis=1, concat_axis=1, tiled=True)
    returned = jnp.roll(returned, -own_start, axis=1).reshape(slot_count * shard_count, width)
    final = (
        token_rows.astype(jnp.float32) + gate_value[:, None] * returned.astype(jnp.float32)
    ).astype(jnp.bfloat16)
    target = jnp.where(is_valid, kept_idx[0], TOK_DEV)
    return hidden.at[target].set(final, mode="drop")


def solution(mesh):
    placed = (
        P(("groups", "blk"), None),
        P(("groups", "blk"), None),
        P(("groups", "blk")),
        P(),
        P(),
        P(),
        P("blk", None),
        P("blk", None),
        P("blk", None),
        P("blk", None),
    )
    n = mesh.shape["blk"]
    by_heads = n % 4 == 0 and Q_HEADS == 2 * n
    step = functools.partial(body, n) if by_heads else wide_body
    return jax.shard_map(
        step, mesh=mesh, in_specs=placed, out_specs=P(("groups", "blk"), None), check_vma=False
    )
```
